32 devices in a mesh: ma: 8 (over z, y), freq: 4 (over x, core).
Axes of the slice: x: 2, y: 2, z: 4, core: 2. Of those that a mesh axis runs over, the one named last changes fastest.
Arguments:
- visibility: float32 [2, 128, 16, 12288], P(None, None, 'ma', 'freq'), may hold values from -6 to 6
- svd_ranks: int32 [64], P('freq'), may hold values from 96 to 192, as said below
- kl_basis: bfloat16 [2, 12288, 1024], P(None, 'freq'), may hold values from -0.0390625 to 0.0390625
- weight_table: float32 [8, 1024], replicated, may hold values from 0.5 to 5
- seed_labels: int32 [128], replicated, may hold values from 0 to 7
Outputs:
- time_series: float32 [2, 128, 16, 12288], P(None, 'ma', None, 'freq')
The draws below stay inside these ranges and needn't reach their ends.
Inputs may be any that keep to these rules, and one draw needn't show every extreme that they name: `svd_ranks`: some frequency has all 192 components.
All inputs are finite; a program needn't handle non-finite values.
Results may differ from the reference program's by a relative error of at most 0.004.
Values may be sent and summed in bfloat16 or wider, within the bound.
No kernel may reach another device: no remote copies, remote signals or barrier semaphores. Data moves between devices by JAX's collectives and lax.ppermute only.
A program may use at most 64 MiB of HBM per device.

```python
import math
import jax
import jax.numpy as jnp
from jax import lax

S = 192
FREQS = 64
KMODES = 1024
SETS = 8
REALS = 128
M = 16


def draw_svd_ranks(key, part):
    first_key = jax.random.fold_in(key, 11)
    second_key = jax.random.fold_in(key, 23)
    drawn = jax.random.randint(first_key, (FREQS,), S // 2, S + 1, dtype=jnp.int32)
    chosen = jax.random.randint(second_key, (), 0, FREQS, dtype=jnp.int32)
    return drawn.at[chosen].set(S)


def with_ends(array, key, least, high):
    longest = array.shape.index(max(array.shape))
    spots = []
    for shift in (0, 1):
        where = [jax.random.randint(jax.random.fold_in(key, axis), (), 0, length) for axis, length in enumerate(array.shape)]
        where[longest] = (where[longest] + shift) % array.shape[longest]
        spots.append(tuple(where))
    return array.at[spots[0]].set(least).at[spots[1]].set(high)


def levels(rng, extent, pieces, least, top_value):
    def one(dim, shards_of):
        draws = jax.random.uniform(jax.random.fold_in(jax.random.fold_in(rng, 6), dim), (shards_of,), jnp.float32, least / len(pieces), top_value / len(pieces))
        return jnp.repeat(jnp.exp(draws), extent[dim] // shards_of).reshape((-1,) + (1,) * (len(extent) - dim - 1))

    level = one(*pieces[0])
    for cut in pieces[1:]:
        level = level * one(*cut)
    return level


def noise(rng, shape, spread, bound, split=(), held_as=jnp.bfloat16):
    array = jax.random.normal(rng, shape, jnp.float32) * spread
    if len(split) > 0:
        array = levels(rng, shape, split, -0.22, 0.18) * array
    return jnp.clip(array, min=-bound, max=bound).astype(held_as)


def setup_inputs(seed: int = 0) -> dict:
    streams_of = jax.random.split(jax.random.key(seed), 6)
    return {
        "visibility": noise(streams_of[0], (2, REALS, M, FREQS * S), 1.0, 6.0, ((2, 8), (3, 4)), jnp.float32),
        "svd_ranks": draw_svd_ranks(jax.random.fold_in(streams_of[5], 71), 0),
        "kl_basis": noise(streams_of[2], (2, FREQS * S, KMODES), (2 * FREQS * S) ** -0.5, 0.0390625, ((1, 4),)),
        "weight_table": jnp.clip(jnp.exp(jax.random.uniform(streams_of[3], (SETS, KMODES), jnp.float32, math.log(0.5), math.log(5.0))), 0.5, 5.0),
        "seed_labels": with_ends(jax.random.randint(streams_of[4], (REALS,), 0, SETS), jax.random.fold_in(streams_of[4], 1), 0, SETS - 1).astype(jnp.int32),
    }


def reference(visibility, svd_ranks, kl_basis, weight_table, seed_labels):
    column_mask = (jnp.arange(S, dtype=jnp.int32)[None, :] < svd_ranks[:, None]).astype(jnp.float32).reshape(-1)
    masked = (visibility * column_mask).astype(jnp.bfloat16)
    row_total = REALS * M
    masked_re = masked[0].reshape(row_total, -1)
    masked_im = masked[1].reshape(row_total, -1)
    basis_re = kl_basis[0]
    basis_im = kl_basis[1]
    modes_re = jnp.dot(masked_re, basis_re, preferred_element_type=jnp.float32) + jnp.dot(masked_im, basis_im, preferred_element_type=jnp.float32)
    modes_im = jnp.dot(masked_im, basis_re, preferred_element_type=jnp.float32) - jnp.dot(masked_re, basis_im, preferred_element_type=jnp.float32)
    row_weights = jnp.repeat(weight_table[seed_labels], M, axis=0)
    coeffs_re = (modes_re * row_weights).astype(jnp.bfloat16)
    coeffs_im = (modes_im * row_weights).astype(jnp.bfloat16)
    fields_re = jnp.dot(coeffs_re, basis_re.T, preferred_element_type=jnp.float32) - jnp.dot(coeffs_im, basis_im.T, preferred_element_type=jnp.float32)
    fields_im = jnp.dot(coeffs_re, basis_im.T, preferred_element_type=jnp.float32) + jnp.dot(coeffs_im, basis_re.T, preferred_element_type=jnp.float32)
    spectrum = lax.complex(fields_re, fields_im).reshape(REALS, M, -1)
    series = jnp.fft.ifft(spectrum, axis=1) * math.sqrt(M)
    return jnp.stack([jnp.real(series), jnp.imag(series)]).astype(jnp.float32)
```

```python
import functools
import math

import jax
import jax.numpy as jnp
from jax import lax
from jax.experimental import pallas as pl
from jax.experimental.pallas import tpu as pltpu
from jax.sharding import PartitionSpec as P


LANES = 128
BF16 = jnp.bfloat16
F32 = jnp.float32
MIB = 1 << 20


def swap(array, axis, bit):
    size = lax.axis_size(axis)
    return lax.ppermute(array, axis, [(i, i ^ bit) for i in range(size)])


def mask_row(ranks, tile, rank_width):
    start = tile * LANES
    freq = start // rank_width
    offset = start - freq * rank_width
    following = jnp.minimum(freq + 1, ranks.shape[0] - 1)
    step = offset + lax.broadcasted_iota(jnp.int32, (1, LANES), 1)
    limit = jnp.where(step < rank_width, ranks[freq], ranks[following] + rank_width)
    return jnp.where(step < limit, 1.0, 0.0).astype(F32)


def first_kernel(ranks, where, vis, basis, rows_out, send_out, total, *, reals, rank_width, tiles):
    step = pl.program_id(0)
    half = reals * 2
    flat = vis.reshape(vis.shape[0] * vis.shape[1], LANES)
    stride = vis.shape[1]
    for tile in range(tiles):
        mask = mask_row(ranks, step * tiles + tile, rank_width)
        lanes = slice(tile * LANES, (tile + 1) * LANES)
        for part in range(2):
            for m in range(2):
                start = part * reals * stride + tile * 2 + m
                block = flat[pl.ds(start, reals, stride=stride), :] * mask
                low = part * half + m * reals
                rows_out[low : low + reals, lanes] = block.astype(BF16)
                if part == 0:
                    rows_out[2 * half + low : 2 * half + low + reals, lanes] = (-block).astype(BF16)
    product = jnp.dot(rows_out[: 2 * half, :], basis[0], preferred_element_type=F32)
    product += jnp.dot(rows_out[half:, :], basis[1], preferred_element_type=F32)

    @pl.when(step == 0)
    def _():
        total[...] = product

    @pl.when(step > 0)
    def _():
        total[...] += product

    @pl.when(step == pl.num_programs(0) - 1)
    def _():
        send_out[...] = total[...]


def project_first(vis, ranks, where, basis, width):
    _, reals, _, columns = vis.shape
    tiles = 4
    chunk = tiles * LANES
    view = vis.reshape(2, reals, 2, columns // LANES, LANES).transpose(0, 1, 3, 2, 4)
    view = view.reshape(2 * reals, columns // LANES * 2, LANES)
    view = pltpu.with_memory_space_constraint(view, pltpu.HBM)
    rows = 2 * reals
    kernel = functools.partial(
        first_kernel, reals=reals, rank_width=columns // ranks.shape[0], tiles=tiles
    )
    return pl.pallas_call(
        kernel,
        grid_spec=pltpu.PrefetchScalarGridSpec(
            num_scalar_prefetch=2,
            grid=(columns // chunk,),
            in_specs=[
                pl.BlockSpec((2 * reals, 2 * tiles, LANES), lambda i, r, w: (0, i, 0)),
                pl.BlockSpec((2, chunk, width), lambda i, r, w: (0, i, w[0])),
            ],
            out_specs=[
                pl.BlockSpec((3 * rows, chunk), lambda i, r, w: (0, i)),
                pl.BlockSpec((2 * rows, width), lambda i, r, w: (0, 0)),
            ],
            scratch_shapes=[pltpu.VMEM((2 * rows, width), F32)],
        ),
        out_shape=[
            jax.ShapeDtypeStruct((3 * rows, columns), BF16),
            jax.ShapeDtypeStruct((2 * rows, width), F32),
        ],
        compiler_params=pltpu.CompilerParams(vmem_limit_bytes=24 * MIB),
        cost_estimate=pl.CostEstimate(
            flops=8 * rows * columns * width,
            bytes_accessed=vis.size * 4 + columns * width * 4,
            transcendentals=0,
        ),
        name="project_first",
    )(ranks, where, view, basis)


def again_kernel(where, rows_in, basis, out, total):
    step = pl.program_id(0)
    half = rows_in.shape[0] // 3
    product = jnp.dot(rows_in[: 2 * half, :], basis[0], preferred_element_type=F32)
    product += jnp.dot(rows_in[half:, :], basis[1], preferred_element_type=F32)

    @pl.when(step == 0)
    def _():
        total[...] = product

    @pl.when(step > 0)
    def _():
        total[...] += product

    @pl.when(step == pl.num_programs(0) - 1)
    def _():
        out[...] = total[...]


def project_again(rows_in, where, basis, width):
    rows3, columns = rows_in.shape
    rows = rows3 // 3
    chunk = columns // 3 if columns % (3 * LANES) == 0 else columns
    return pl.pallas_call(
        again_kernel,
        grid_spec=pltpu.PrefetchScalarGridSpec(
            num_scalar_prefetch=1,
            grid=(columns // chunk,),
            in_specs=[
                pl.BlockSpec((rows3, chunk), lambda i, w: (0, i)),
                pl.BlockSpec((2, chunk, width), lambda i, w: (0, i, w[0])),
            ],
            out_specs=pl.BlockSpec((2 * rows, width), lambda i, w: (0, 0)),
            scratch_shapes=[pltpu.VMEM((2 * rows, width), F32)],
        ),
        out_shape=jax.ShapeDtypeStruct((2 * rows, width), F32),
        compiler_params=pltpu.CompilerParams(vmem_limit_bytes=24 * MIB),
        cost_estimate=pl.CostEstimate(
            flops=8 * rows * columns * width,
            bytes_accessed=rows_in.size * 2 + columns * width * 4,
            transcendentals=0,
        ),
        name="project_again",
    )(where, rows_in, basis)


def weight_kernel(own, core_part, chip_part, weights, out, *, blocks, width_at):
    rows = own.shape[0] // 4
    per = rows // blocks
    for part in range(2):
        for m in range(2):
            low = (part * 2 + m) * rows
            total = own[low : low + rows, :] + core_part[low : low + rows, :]
            total = total + chip_part[low : low + rows, :].astype(F32)
            value = (total * weights[...]).astype(BF16)
            for block in range(blocks):
                out[block, (part * 2 + m) * per : (part * 2 + m + 1) * per, :] = value[
                    block * per : (block + 1) * per, :
                ]


def apply_weights(own, core_half, where, chip_part, weights, blocks):
    rows, width = own.shape
    per = rows // blocks
    return pl.pallas_call(
        lambda w, *refs: weight_kernel(*refs, blocks=blocks, width_at=0),
        grid_spec=pltpu.PrefetchScalarGridSpec(
            num_scalar_prefetch=1,
            grid=(1,),
            in_specs=[
                pl.BlockSpec((rows, width), lambda i, w: (0, 0)),
                pl.BlockSpec((rows, width), lambda i, w: (0, w[0])),
                pl.BlockSpec((rows, width), lambda i, w: (0, 0)),
                pl.BlockSpec(weights.shape, lambda i, w: (0, 0)),
            ],
            out_specs=pl.BlockSpec((blocks, per, width), lambda i, w: (0, 0, 0)),
        ),
        out_shape=jax.ShapeDtypeStruct((blocks, per, width), BF16),
        compiler_params=pltpu.CompilerParams(vmem_limit_bytes=8 * MIB),
        name="apply_weights",
    )(where, own, core_half, chip_part, weights)


def add_kernel(w, own, core_part, out):
    out[...] = (own[...] + core_part[...]).astype(BF16)


def add_parts(own, core_half, where):
    rows, width = own.shape
    return pl.pallas_call(
        add_kernel,
        grid_spec=pltpu.PrefetchScalarGridSpec(
            num_scalar_prefetch=1,
            grid=(1,),
            in_specs=[
                pl.BlockSpec((rows, width), lambda i, w: (0, 0)),
                pl.BlockSpec((rows, width), lambda i, w: (0, w[0])),
            ],
            out_specs=pl.BlockSpec((rows, width), lambda i, w: (0, 0)),
        ),
        out_shape=jax.ShapeDtypeStruct((rows, width), BF16),
        compiler_params=pltpu.CompilerParams(vmem_limit_bytes=8 * MIB),
        name="add_parts",
    )(where, own, core_half)


def butterfly(a, b, c, d):
    s_re, s_im = a[0] + c[0], a[1] + c[1]
    d_re, d_im = a[0] - c[0], a[1] - c[1]
    t_re, t_im = b[0] + d[0], b[1] + d[1]
    e_re, e_im = b[0] - d[0], b[1] - d[1]
    return (
        (s_re + t_re, s_im + t_im),
        (d_re - e_im, d_im + e_re),
        (s_re - t_re, s_im - t_im),
        (d_re + e_im, d_im - e_re),
    )


def twiddle(value, index, scale):
    re, im = value
    quarter = index % 16
    cosine = math.cos(2 * math.pi * quarter / 16) * scale
    sine = math.sin(2 * math.pi * quarter / 16) * scale
    if quarter == 0:
        return (re * scale, im * scale)
    if quarter == 4:
        return (im * -scale, re * scale)
    if quarter == 2:
        return ((re - im) * cosine, (re + im) * cosine)
    if quarter == 6:
        return ((re + im) * cosine, (re - im) * sine)
    return (re * cosine - im * sine, re * sine + im * cosine)


def transform(values):
    inner = []
    for m1 in range(4):
        outs = butterfly(*[values[m1 + 4 * m0] for m0 in range(4)])
        inner.append([twiddle(outs[t0], m1 * t0, 0.25) for t0 in range(4)])
    result = [None] * 16
    for t0 in range(4):
        outs = butterfly(*[inner[m1][t0] for m1 in range(4)])
        for t1 in range(4):
            result[4 * t1 + t0] = outs[t1]
    return result


def field_kernel(where, *refs, pieces, blocks):
    coeffs = refs[:pieces]
    bases = refs[pieces : 2 * pieces]
    out, rows, fields = refs[2 * pieces :]
    step = pl.program_id(0)
    per = coeffs[0].shape[1] // 4
    width = coeffs[0].shape[2]
    half = blocks * 2 * per

    @pl.when(step == 0)
    def _():
        for piece in range(pieces):
            lanes = slice(piece * width, (piece + 1) * width)
            for block in range(blocks):
                low = block * 2 * per
                re = coeffs[piece][block, : 2 * per, :]
                im = coeffs[piece][block, 2 * per :, :]
                rows[low : low + 2 * per, lanes] = -im
                rows[half + low : half + low + 2 * per, lanes] = re
                rows[2 * half + low : 2 * half + low + 2 * per, lanes] = im

    contract = (((1,), (1,)), ((), ()))
    total = None
    for piece in range(pieces):
        lanes = slice(piece * width, (piece + 1) * width)
        term = lax.dot_general(
            rows[half:, lanes], bases[piece][0], contract, preferred_element_type=F32
        )
        total = term if total is None else total + term
        total += lax.dot_general(
            rows[: 2 * half, lanes], bases[piece][1], contract, preferred_element_type=F32
        )
    tile_count = fields.shape[0]
    for tile in range(tile_count):
        fields[tile] = total[:, tile * LANES : (tile + 1) * LANES]
    points = 2 * blocks
    out_rows = out.shape[1] * tile_count
    flat = out.reshape(2 * out_rows * 8, LANES)
    for tile in range(tile_count):
        for group in range(per // 8):
            values = []
            for m in range(points):
                low = m * per + group * 8
                values.append(
                    (fields[tile, low : low + 8, :], fields[tile, half + low : half + low + 8, :])
                )
            series = transform(values)
            for t in range(points):
                for part in range(2):
                    first = part * out_rows + (group * 8 * points + t) // 8 * tile_count
                    flat[pl.ds((first + tile) * 8 + t % 8, 8, stride=points * tile_count), :] = (
                        series[t][part]
                    )


def make_fields(coeffs, where, basis, reals_dev, tile):
    pieces = len(coeffs)
    blocks, per4, width = coeffs[0].shape
    columns = basis.shape[1]
    rows = blocks * per4 // 2
    per = per4 // 4
    in_specs = [pl.BlockSpec((blocks, per4, width), lambda i, w: (0, 0, 0))] * pieces
    for piece in range(pieces):
        in_specs.append(
            pl.BlockSpec((2, tile, width), lambda i, w, piece=piece: (0, i, w[piece]))
        )
    tiled = pl.pallas_call(
        functools.partial(field_kernel, pieces=pieces, blocks=blocks),
        grid_spec=pltpu.PrefetchScalarGridSpec(
            num_scalar_prefetch=1,
            grid=(columns // tile,),
            in_specs=in_specs,
            out_specs=pl.BlockSpec(
                (2, rows // 8, tile // LANES, 8, LANES), lambda i, w: (0, 0, i, 0, 0)
            ),
            scratch_shapes=[
                pltpu.VMEM((3 * rows, pieces * width), BF16),
                pltpu.VMEM((tile // LANES, 2 * rows, LANES), F32),
            ],
        ),
        out_shape=jax.ShapeDtypeStruct((2, rows // 8, columns // LANES, 8, LANES), F32),
        compiler_params=pltpu.CompilerParams(vmem_limit_bytes=32 * MIB),
        cost_estimate=pl.CostEstimate(
            flops=8 * rows * columns * width * pieces,
            bytes_accessed=columns * width * pieces * 4 + rows * columns * 8,
            transcendentals=0,
        ),
        name="make_fields",
    )(where, *coeffs, *([basis] * pieces))
    return tiled.transpose(0, 1, 3, 2, 4).reshape(2, rows, columns)


def fast_shards(visibility, svd_ranks, kl_basis, weight_table, seed_labels):
    _, reals, _, columns = visibility.shape
    modes = kl_basis.shape[2]
    blocks = lax.axis_size("ma")
    index = lax.axis_index("freq")
    core, chip = index & 1, index >> 1
    kl_basis = pltpu.with_memory_space_constraint(kl_basis, pltpu.HBM)
    half, width = modes // 2, modes // 4
    mine = core * 2 + chip
    one = lambda value: value[None].astype(jnp.int32)

    rows, away = project_first(visibility, svd_ranks, one(1 - core), kl_basis, half)
    core_half = swap(away, "freq", 1)
    chip_own = project_again(rows, one(core * 2 + 1 - chip), kl_basis, width)
    chip_send = add_parts(chip_own, core_half, one(1 - chip))
    chip_part = swap(chip_send, "freq", 2)
    own = project_again(rows, one(mine), kl_basis, width)

    table = lax.dynamic_slice_in_dim(weight_table, mine * width, width, 1)
    sets = jnp.arange(weight_table.shape[0], dtype=jnp.int32)
    one_hot = (seed_labels[:, None] == sets[None, :]).astype(F32)
    weights = jnp.dot(one_hot, table, precision=lax.Precision.HIGHEST)
    coeffs = apply_weights(own, core_half, one(chip), chip_part, weights, blocks)

    coeffs = lax.all_to_all(coeffs, "ma", split_axis=0, concat_axis=0, tiled=True)
    from_core = swap(coeffs, "freq", 1)
    from_chip = swap(coeffs, "freq", 2)
    from_both = swap(from_chip, "freq", 1)
    order = jnp.stack([mine, (1 - core) * 2 + chip, core * 2 + 1 - chip, (1 - core) * 2 + 1 - chip])
    series = make_fields(
        [coeffs, from_core, from_chip, from_both], order.astype(jnp.int32), kl_basis, reals // blocks, 512
    )
    return series.reshape(2, reals // blocks, 2 * blocks, columns)


def plain_shards(visibility, svd_ranks, kl_basis, weight_table, seed_labels):
    _, reals, local_m, columns = visibility.shape
    rank_width = columns // svd_ranks.shape[0]
    steps = jnp.arange(rank_width, dtype=jnp.int32)
    mask = (steps[None, :] < svd_ranks[:, None]).astype(F32).reshape(1, 1, 1, columns)
    masked = (visibility * mask).astype(BF16).reshape(2, reals * local_m, columns)

    def product(matrix, signal):
        return lax.dot_general(
            matrix, signal, (((0,), (1,)), ((), ())), preferred_element_type=F32
        )

    modes_re = product(kl_basis[0], masked[0]) + product(kl_basis[1], masked[1])
    modes_im = product(kl_basis[0], masked[1]) - product(kl_basis[1], masked[0])
    parts = jnp.stack([modes_re, modes_im], axis=1)
    summed = lax.psum_scatter(parts, "freq", scatter_dimension=0, tiled=True)
    held = summed.shape[0]
    table = lax.dynamic_slice_in_dim(weight_table, lax.axis_index("freq") * held, held, 1)
    labels = jnp.repeat(seed_labels, local_m)
    sets = jnp.arange(weight_table.shape[0], dtype=jnp.int32)
    one_hot = (sets[:, None] == labels[None, :]).astype(F32)
    weights = lax.dot_general(
        table, one_hot, (((0,), (0,)), ((), ())), precision=lax.Precision.HIGHEST
    )
    coeffs = (summed * weights[:, None, :]).astype(BF16)
    coeffs = lax.all_to_all(
        coeffs.reshape(held, 2, reals, local_m), "ma", split_axis=2, concat_axis=3, tiled=True
    ).reshape(held, 2, -1)
    coeffs = lax.all_gather(coeffs, "freq", axis=0, tiled=True)
    fields_re = product(coeffs[:, 0], kl_basis[0]) - product(coeffs[:, 1], kl_basis[1])
    fields_im = product(coeffs[:, 0], kl_basis[1]) + product(coeffs[:, 1], kl_basis[0])
    shape = (reals // lax.axis_size("ma"), -1, columns)
    fields_re, fields_im = fields_re.reshape(shape), fields_im.reshape(shape)
    length = fields_re.shape[1]
    index = jnp.arange(length, dtype=jnp.int32)
    angles = (index[:, None] * index[None, :] % length).astype(F32) * (2.0 * math.pi / length)
    cosine = jnp.cos(angles) / math.sqrt(length)
    sine = jnp.sin(angles) / math.sqrt(length)

    def apply(matrix, signal):
        return jnp.einsum("tm,rmc->rtc", matrix, signal, precision=lax.Precision.HIGHEST)

    return jnp.stack(
        [
            apply(cosine, fields_re) - apply(sine, fields_im),
            apply(sine, fields_re) + apply(cosine, fields_im),
        ]
    )


def fits(mesh, visibility, svd_ranks, kl_basis):
    blocks, freq = mesh.shape["ma"], mesh.shape["freq"]
    _, reals, points, columns = visibility.shape
    rank_width = columns // svd_ranks.shape[0]
    return (
        freq == 4
        and points == 16
        and points == 2 * blocks
        and reals % (16 * blocks) == 0
        and rank_width >= LANES
        and columns // freq % (4 * LANES) == 0
        and kl_basis.shape[2] % (4 * LANES) == 0
    )


def solution(mesh):
    in_specs = (P(None, None, "ma", "freq"), P("freq"), P(None, "freq", None), P(), P())
    out_specs = P(None, "ma", None, "freq")

    def program(visibility, svd_ranks, kl_basis, weight_table, seed_labels):
        body = fast_shards if fits(mesh, visibility, svd_ranks, kl_basis) else plain_shards
        return jax.shard_map(
            body, mesh=mesh, in_specs=in_specs, out_specs=out_specs, check_vma=False
        )(visibility, svd_ranks, kl_basis, weight_table, seed_labels)

    return program
```

```python
import functools
import math

import jax
import jax.numpy as jnp
from jax import lax
from jax.experimental import pallas as pl
from jax.experimental.pallas import tpu as pltpu
from jax.sharding import PartitionSpec as P


LANES = 128
BF16 = jnp.bfloat16
F32 = jnp.float32
MIB = 1 << 20
HBM = pl.BlockSpec(memory_space=pltpu.HBM)
VMEM = pl.BlockSpec(memory_space=pltpu.VMEM)
SMEM = pl.BlockSpec(memory_space=pltpu.SMEM)


def in_hbm(array):
    return pltpu.with_memory_space_constraint(array, pltpu.HBM)


def swap(array, axis, bit):
    size = lax.axis_size(axis)
    return lax.ppermute(array, axis, [(i, i ^ bit) for i in range(size)])


def mask_row(ranks, tile, rank_width):
    start = tile * LANES
    freq = start // rank_width
    offset = start - freq * rank_width
    following = jnp.minimum(freq + 1, ranks.shape[0] - 1)
    step = offset + lax.broadcasted_iota(jnp.int32, (1, LANES), 1)
    limit = jnp.where(step < rank_width, ranks[freq], ranks[following] + rank_width)
    return jnp.where(step < limit, 1.0, 0.0).astype(F32)


def both_parts(rows):
    half = rows.shape[0] // 2
    re, im = rows[:half, :], rows[half:, :]
    turned = jnp.concatenate([im, -re], axis=0)
    return jnp.concatenate([rows[...], turned], axis=1)


def first_kernel(ranks, where, vis, basis, rows_out, send, rows, vis_held, basis_held, sems, *, reals, rank_width):
    chunks, _, stride, _ = vis_held.shape
    chunk, width = basis_held.shape[2:]
    tiles = chunk // LANES
    half = 2 * reals
    first_mode = pl.multiple_of(where[0] * width, width)
    copies = []
    for i in range(chunks):
        copies.append(
            (
                pltpu.make_async_copy(
                    vis.at[:, pl.ds(i * stride, stride), :], vis_held.at[i], sems.at[0, i]
                ),
                pltpu.make_async_copy(
                    basis.at[:, pl.ds(i * chunk, chunk), pl.ds(first_mode, width)],
                    basis_held.at[i],
                    sems.at[1, i],
                ),
                pltpu.make_async_copy(rows.at[i], rows_out.at[i], sems.at[2, i]),
            )
        )
        for copy in copies[-1][:2]:
            copy.start()

    def mask_chunk(i):
        copies[i][0].wait()
        flat = vis_held.at[i].reshape(half * stride, LANES)
        for tile in range(tiles):
            mask = mask_row(ranks, i * tiles + tile, rank_width)
            lanes = slice(tile * LANES, (tile + 1) * LANES)
            for part in range(2):
                for m in range(2):
                    start = part * reals * stride + tile * 2 + m
                    block = flat[pl.ds(start, reals, stride=stride), :] * mask
                    low = part * half + m * reals
                    rows[i, low : low + reals, lanes] = block.astype(BF16)

    mask_chunk(0)
    for i in range(chunks):
        if i + 1 < chunks:
            mask_chunk(i + 1)
        copies[i][1].wait()
        product = jnp.dot(
            both_parts(rows.at[i]),
            basis_held[i].reshape(2 * chunk, width),
            preferred_element_type=F32,
        )
        if i == 0:
            send[...] = product
        else:
            send[...] += product
        copies[i][2].start()
    for i in range(chunks):
        copies[i][2].wait()


def project_first(vis, ranks, where, basis, width):
    _, reals, _, columns = vis.shape
    chunk = 4 * LANES
    chunks = columns // chunk
    view = vis.reshape(2, reals, 2, columns // LANES, LANES).transpose(0, 1, 3, 2, 4)
    view = view.reshape(2 * reals, columns // LANES * 2, LANES)
    rows = 2 * reals
    return pl.pallas_call(
        functools.partial(first_kernel, reals=reals, rank_width=columns // ranks.shape[0]),
        in_specs=[SMEM, SMEM, HBM, HBM],
        out_specs=[HBM, VMEM],
        scratch_shapes=[
            pltpu.VMEM((chunks, 2 * rows, chunk), BF16),
            pltpu.VMEM((chunks, 2 * reals, 2 * chunk // LANES, LANES), F32),
            pltpu.VMEM((chunks, 2, chunk, width), BF16),
            pltpu.SemaphoreType.DMA((3, chunks)),
        ],
        out_shape=[
            pltpu.HBM((chunks, 2 * rows, chunk), BF16),
            jax.ShapeDtypeStruct((2 * rows, width), F32),
        ],
        compiler_params=pltpu.CompilerParams(vmem_limit_bytes=24 * MIB),
        cost_estimate=pl.CostEstimate(
            flops=8 * rows * columns * width,
            bytes_accessed=vis.size * 4 + columns * width * 4 + rows * columns * 4,
            transcendentals=0,
        ),
        name="project_first",
    )(in_hbm(ranks), where, in_hbm(view), in_hbm(basis))


def again_kernel(where, rows, basis, out, rows_held, basis_held, sems):
    chunks, _, chunk, width = basis_held.shape
    first_mode = pl.multiple_of(where[0] * width, width)
    copies = []
    for i in range(chunks):
        copies.append(
            (
                pltpu.make_async_copy(rows.at[i], rows_held.at[i], sems.at[0, i]),
                pltpu.make_async_copy(
                    basis.at[:, pl.ds(i * chunk, chunk), pl.ds(first_mode, width)],
                    basis_held.at[i],
                    sems.at[1, i],
                ),
            )
        )
        for copy in copies[-1]:
            copy.start()
    for i in range(chunks):
        for copy in copies[i]:
            copy.wait()
        product = jnp.dot(
            both_parts(rows_held.at[i]),
            basis_held[i].reshape(2 * chunk, width),
            preferred_element_type=F32,
        )
        if i == 0:
            out[...] = product
        else:
            out[...] += product


def project_again(rows, where, basis, width):
    chunks, rows2, chunk = rows.shape
    return pl.pallas_call(
        again_kernel,
        in_specs=[SMEM, HBM, HBM],
        out_specs=VMEM,
        scratch_shapes=[
            pltpu.VMEM((chunks, rows2, chunk), BF16),
            pltpu.VMEM((chunks, 2, chunk, width), BF16),
            pltpu.SemaphoreType.DMA((2, chunks)),
        ],
        out_shape=jax.ShapeDtypeStruct((rows2, width), F32),
        compiler_params=pltpu.CompilerParams(vmem_limit_bytes=12 * MIB),
        cost_estimate=pl.CostEstimate(
            flops=4 * rows2 * chunks * chunk * width,
            bytes_accessed=rows.size * 2 + chunks * chunk * width * 4,
            transcendentals=0,
        ),
        name="project_again",
    )(where, in_hbm(rows), in_hbm(basis))


def weight_kernel(own, core_part, chip_part, weights, out, *, blocks, width_at):
    rows = own.shape[0] // 4
    per = rows // blocks
    for part in range(2):
        for m in range(2):
            low = (part * 2 + m) * rows
            total = own[low : low + rows, :] + core_part[low : low + rows, :]
            total = total + chip_part[low : low + rows, :].astype(F32)
            value = (total * weights[...]).astype(BF16)
            for block in range(blocks):
                out[block, (part * 2 + m) * per : (part * 2 + m + 1) * per, :] = value[
                    block * per : (block + 1) * per, :
                ]


def apply_weights(own, core_half, where, chip_part, weights, blocks):
    rows, width = own.shape
    per = rows // blocks
    return pl.pallas_call(
        lambda w, *refs: weight_kernel(*refs, blocks=blocks, width_at=0),
        grid_spec=pltpu.PrefetchScalarGridSpec(
            num_scalar_prefetch=1,
            grid=(1,),
            in_specs=[
                pl.BlockSpec((rows, width), lambda i, w: (0, 0)),
                pl.BlockSpec((rows, width), lambda i, w: (0, w[0])),
                pl.BlockSpec((rows, width), lambda i, w: (0, 0)),
                pl.BlockSpec(weights.shape, lambda i, w: (0, 0)),
            ],
            out_specs=pl.BlockSpec((blocks, per, width), lambda i, w: (0, 0, 0)),
        ),
        out_shape=jax.ShapeDtypeStruct((blocks, per, width), BF16),
        compiler_params=pltpu.CompilerParams(vmem_limit_bytes=8 * MIB),
        name="apply_weights",
    )(where, own, core_half, chip_part, weights)


def add_kernel(w, own, core_part, out):
    out[...] = (own[...] + core_part[...]).astype(BF16)


def add_parts(own, core_half, where):
    rows, width = own.shape
    return pl.pallas_call(
        add_kernel,
        grid_spec=pltpu.PrefetchScalarGridSpec(
            num_scalar_prefetch=1,
            grid=(1,),
            in_specs=[
                pl.BlockSpec((rows, width), lambda i, w: (0, 0)),
                pl.BlockSpec((rows, width), lambda i, w: (0, w[0])),
            ],
            out_specs=pl.BlockSpec((rows, width), lambda i, w: (0, 0)),
        ),
        out_shape=jax.ShapeDtypeStruct((rows, width), BF16),
        compiler_params=pltpu.CompilerParams(vmem_limit_bytes=8 * MIB),
        name="add_parts",
    )(where, own, core_half)


def butterfly(a, b, c, d):
    s_re, s_im = a[0] + c[0], a[1] + c[1]
    d_re, d_im = a[0] - c[0], a[1] - c[1]
    t_re, t_im = b[0] + d[0], b[1] + d[1]
    e_re, e_im = b[0] - d[0], b[1] - d[1]
    return (
        (s_re + t_re, s_im + t_im),
        (d_re - e_im, d_im + e_re),
        (s_re - t_re, s_im - t_im),
        (d_re + e_im, d_im - e_re),
    )


def twiddle(value, index, scale):
    re, im = value
    quarter = index % 16
    cosine = math.cos(2 * math.pi * quarter / 16) * scale
    sine = math.sin(2 * math.pi * quarter / 16) * scale
    if quarter == 0:
        return (re * scale, im * scale)
    if quarter == 4:
        return (im * -scale, re * scale)
    if quarter == 2:
        return ((re - im) * cosine, (re + im) * cosine)
    if quarter == 6:
        return ((re + im) * cosine, (re - im) * sine)
    return (re * cosine - im * sine, re * sine + im * cosine)


def transform(values):
    inner = []
    for m1 in range(4):
        outs = butterfly(*[values[m1 + 4 * m0] for m0 in range(4)])
        inner.append([twiddle(outs[t0], m1 * t0, 0.25) for t0 in range(4)])
    result = [None] * 16
    for t0 in range(4):
        outs = butterfly(*[inner[m1][t0] for m1 in range(4)])
        for t1 in range(4):
            result[4 * t1 + t0] = outs[t1]
    return result


def transform_kernel(coeffs, out, moved):
    blocks, per4, width = coeffs.shape
    per = per4 // 4
    points = 2 * blocks
    rows = per * points
    for lane_tile in range(width // LANES):
        lanes = slice(lane_tile * LANES, (lane_tile + 1) * LANES)
        loaded = []
        for m in range(points):
            low = m % 2 * per
            loaded.append(
                [
                    coeffs[m // 2, part * 2 * per + low : part * 2 * per + low + per, lanes].astype(F32)
                    for part in range(2)
                ]
            )
        result = transform(loaded)
        for t in range(points):
            for part in range(2):
                moved[lane_tile, pl.ds(part * rows + t, per, stride=points), :] = result[t][part]
        for part in range(2):
            out[part, :, lanes] = moved[lane_tile, part * rows : (part + 1) * rows, :].astype(BF16)


def to_times(coeffs):
    blocks, per4, width = coeffs.shape
    rows = blocks * per4 // 2
    return pl.pallas_call(
        transform_kernel,
        in_specs=[VMEM],
        out_specs=VMEM,
        scratch_shapes=[pltpu.VMEM((width // LANES, 2 * rows, LANES), F32)],
        out_shape=jax.ShapeDtypeStruct((2, rows, width), BF16),
        compiler_params=pltpu.CompilerParams(vmem_limit_bytes=8 * MIB),
        name="to_times",
    )(coeffs)


def place_rows(rows, coeffs):
    half = rows.shape[0] // 2
    for piece, coeff in enumerate(coeffs):
        width = coeff.shape[2]
        first = slice(2 * piece * width, (2 * piece + 1) * width)
        second = slice((2 * piece + 1) * width, (2 * piece + 2) * width)
        re, im = coeff[0], coeff[1]
        rows[:half, first] = re
        rows[:half, second] = -im
        rows[half:, first] = im
        rows[half:, second] = re


def start_basis(where, basis, held, sems, tile_index, pieces):
    _, tile, width = held.shape[2:]
    copies = []
    for piece in pieces:
        first_mode = pl.multiple_of(where[piece] * width, width)
        copy = pltpu.make_async_copy(
            basis.at[:, pl.ds(tile_index * tile, tile), pl.ds(first_mode, width)],
            held.at[tile_index, piece],
            sems.at[tile_index, piece],
        )
        copy.start()
        copies.append(copy)
    return copies


def field_tile(rows, held, tile_index, pieces):
    right = jnp.concatenate(
        [held[tile_index, piece, part] for piece in pieces for part in range(2)], axis=1
    )
    depth = held.shape[4] * 2
    left = rows[:, pieces[0] * depth : (pieces[-1] + 1) * depth]
    return lax.dot_general(left, right, (((1,), (1,)), ((), ())), preferred_element_type=F32)


def part_kernel(where, *refs, pieces):
    coeffs = refs[:pieces]
    basis, *out, rows, held, sems = refs[pieces:]
    every = range(pieces)
    copies = [start_basis(where, basis, held, sems, i, every) for i in range(len(out))]
    place_rows(rows, coeffs)
    for i, target in enumerate(out):
        for copy in copies[i]:
            copy.wait()
        target[...] = field_tile(rows, held, i, every)


def make_part(coeffs, where, basis, tile, tiles):
    pieces = len(coeffs)
    _, rows, width = coeffs[0].shape
    return pl.pallas_call(
        functools.partial(part_kernel, pieces=pieces),
        in_specs=[SMEM] + [VMEM] * pieces + [HBM],
        out_specs=[VMEM] * tiles,
        scratch_shapes=[
            pltpu.VMEM((2 * rows, 2 * pieces * width), BF16),
            pltpu.VMEM((tiles, pieces, 2, tile, width), BF16),
            pltpu.SemaphoreType.DMA((tiles, pieces)),
        ],
        out_shape=[jax.ShapeDtypeStruct((2 * rows, tile), F32)] * tiles,
        compiler_params=pltpu.CompilerParams(vmem_limit_bytes=12 * MIB),
        cost_estimate=pl.CostEstimate(
            flops=8 * rows * tiles * tile * width * pieces,
            bytes_accessed=tiles * tile * width * pieces * 4,
            transcendentals=0,
        ),
        name="make_part",
    )(where, *coeffs, in_hbm(basis))


def series_kernel(where, *refs, pieces, old):
    coeffs = refs[:pieces]
    basis, *partial = refs[pieces:-5]
    out, rows, held, series, sems = refs[-5:]
    tiles, _, _, tile, _ = held.shape
    kept = len(partial)
    half = rows.shape[0] // 2
    copies, sends = [], []
    for i in range(tiles):
        used = range(old if i < kept else 0, pieces)
        copies.append((used, start_basis(where, basis, held, sems, i, used)))
    place_rows(rows, coeffs)
    for i, (used, arrivals) in enumerate(copies):
        for copy in arrivals:
            copy.wait()
        value = field_tile(rows, held, i, used)
        if i < kept:
            value += partial[i][...]
        series[i, 0] = value[:half]
        series[i, 1] = value[half:]
        copy = pltpu.make_async_copy(
            series.at[i], out.at[:, :, pl.ds(i * tile, tile)], sems.at[i, pieces]
        )
        copy.start()
        sends.append(copy)
    for copy in sends:
        copy.wait()


def make_series(coeffs, where, basis, tile, partial, old):
    pieces = len(coeffs)
    _, rows, width = coeffs[0].shape
    columns = basis.shape[1]
    tiles = columns // tile
    return pl.pallas_call(
        functools.partial(series_kernel, pieces=pieces, old=old),
        in_specs=[SMEM] + [VMEM] * pieces + [HBM] + [VMEM] * len(partial),
        out_specs=HBM,
        scratch_shapes=[
            pltpu.VMEM((2 * rows, 2 * pieces * width), BF16),
            pltpu.VMEM((tiles, pieces, 2, tile, width), BF16),
            pltpu.VMEM((tiles, 2, rows, tile), F32),
            pltpu.SemaphoreType.DMA((tiles, pieces + 1)),
        ],
        out_shape=jax.ShapeDtypeStruct((2, rows, columns), F32),
        compiler_params=pltpu.CompilerParams(vmem_limit_bytes=32 * MIB),
        cost_estimate=pl.CostEstimate(
            flops=8 * rows * columns * width * pieces,
            bytes_accessed=columns * width * pieces * 4 + rows * columns * 8,
            transcendentals=0,
        ),
        name="make_series",
    )(where, *coeffs, in_hbm(basis), *partial)


def fast_shards(visibility, svd_ranks, kl_basis, weight_table, seed_labels):
    _, reals, _, columns = visibility.shape
    modes = kl_basis.shape[2]
    blocks = lax.axis_size("ma")
    index = lax.axis_index("freq")
    core, chip = index & 1, index >> 1
    half, width = modes // 2, modes // 4
    mine = core * 2 + chip
    one = lambda value: value[None].astype(jnp.int32)

    rows, away = project_first(visibility, svd_ranks, one(1 - core), kl_basis, half)
    core_half = swap(away, "freq", 1)
    chip_own = project_again(rows, one(core * 2 + 1 - chip), kl_basis, width)
    chip_send = add_parts(chip_own, core_half, one(1 - chip))
    chip_part = swap(chip_send, "freq", 2)
    own = project_again(rows, one(mine), kl_basis, width)

    table = lax.dynamic_slice_in_dim(weight_table, mine * width, width, 1)
    sets = jnp.arange(weight_table.shape[0], dtype=jnp.int32)
    one_hot = (seed_labels[:, None] == sets[None, :]).astype(F32)
    weights = jnp.dot(one_hot, table, precision=lax.Precision.HIGHEST)
    coeffs = apply_weights(own, core_half, one(chip), chip_part, weights, blocks)

    coeffs = lax.all_to_all(coeffs, "ma", split_axis=0, concat_axis=0, tiled=True)
    coeffs = to_times(coeffs)
    from_core = swap(coeffs, "freq", 1)
    from_chip = swap(coeffs, "freq", 2)
    places = jnp.stack(
        [mine, (1 - core) * 2 + chip, core * 2 + 1 - chip, (1 - core) * 2 + 1 - chip]
    ).astype(jnp.int32)
    tile = 4 * LANES
    partial = make_part([coeffs, from_core], places, kl_basis, tile, columns // tile // 2)
    from_chip, partial = lax.optimization_barrier((from_chip, partial))
    from_both = swap(from_chip, "freq", 1)
    series = make_series(
        [coeffs, from_core, from_chip, from_both], places, kl_basis, tile, partial, 2
    )
    return series.reshape(2, reals // blocks, 2 * blocks, columns)


def plain_shards(visibility, svd_ranks, kl_basis, weight_table, seed_labels):
    _, reals, local_m, columns = visibility.shape
    rank_width = columns // svd_ranks.shape[0]
    steps = jnp.arange(rank_width, dtype=jnp.int32)
    mask = (steps[None, :] < svd_ranks[:, None]).astype(F32).reshape(1, 1, 1, columns)
    masked = (visibility * mask).astype(BF16).reshape(2, reals * local_m, columns)

    def product(matrix, signal):
        return lax.dot_general(
            matrix, signal, (((0,), (1,)), ((), ())), preferred_element_type=F32
        )

    modes_re = product(kl_basis[0], masked[0]) + product(kl_basis[1], masked[1])
    modes_im = product(kl_basis[0], masked[1]) - product(kl_basis[1], masked[0])
    parts = jnp.stack([modes_re, modes_im], axis=1)
    summed = lax.psum_scatter(parts, "freq", scatter_dimension=0, tiled=True)
    held = summed.shape[0]
    table = lax.dynamic_slice_in_dim(weight_table, lax.axis_index("freq") * held, held, 1)
    labels = jnp.repeat(seed_labels, local_m)
    sets = jnp.arange(weight_table.shape[0], dtype=jnp.int32)
    one_hot = (sets[:, None] == labels[None, :]).astype(F32)
    weights = lax.dot_general(
        table, one_hot, (((0,), (0,)), ((), ())), precision=lax.Precision.HIGHEST
    )
    coeffs = (summed * weights[:, None, :]).astype(BF16)
    coeffs = lax.all_to_all(
        coeffs.reshape(held, 2, reals, local_m), "ma", split_axis=2, concat_axis=3, tiled=True
    ).reshape(held, 2, -1)
    coeffs = lax.all_gather(coeffs, "freq", axis=0, tiled=True)
    fields_re = product(coeffs[:, 0], kl_basis[0]) - product(coeffs[:, 1], kl_basis[1])
    fields_im = product(coeffs[:, 0], kl_basis[1]) + product(coeffs[:, 1], kl_basis[0])
    shape = (reals // lax.axis_size("ma"), -1, columns)
    fields_re, fields_im = fields_re.reshape(shape), fields_im.reshape(shape)
    length = fields_re.shape[1]
    index = jnp.arange(length, dtype=jnp.int32)
    angles = (index[:, None] * index[None, :] % length).astype(F32) * (2.0 * math.pi / length)
    cosine = jnp.cos(angles) / math.sqrt(length)
    sine = jnp.sin(angles) / math.sqrt(length)

    def apply(matrix, signal):
        return jnp.einsum("tm,rmc->rtc", matrix, signal, precision=lax.Precision.HIGHEST)

    return jnp.stack(
        [
            apply(cosine, fields_re) - apply(sine, fields_im),
            apply(sine, fields_re) + apply(cosine, fields_im),
        ]
    )


def fits(mesh, visibility, svd_ranks, kl_basis):
    blocks, freq = mesh.shape["ma"], mesh.shape["freq"]
    _, reals, points, columns = visibility.shape
    rank_width = columns // svd_ranks.shape[0]
    return (
        freq == 4
        and points == 16
        and points == 2 * blocks
        and reals % (16 * blocks) == 0
        and rank_width >= LANES
        and columns // freq % (4 * LANES) == 0
        and kl_basis.shape[2] % (4 * LANES) == 0
    )


def solution(mesh):
    in_specs = (P(None, None, "ma", "freq"), P("freq"), P(None, "freq", None), P(), P())
    out_specs = P(None, "ma", None, "freq")

    def program(visibility, svd_ranks, kl_basis, weight_table, seed_labels):
        body = fast_shards if fits(mesh, visibility, svd_ranks, kl_basis) else plain_shards
        return jax.shard_map(
            body, mesh=mesh, in_specs=in_specs, out_specs=out_specs, check_vma=False
        )(visibility, svd_ranks, kl_basis, weight_table, seed_labels)

    return program
```

```python
import functools
import math

import jax
import jax.numpy as jnp
from jax import lax
from jax.experimental import pallas as pl
from jax.experimental.pallas import tpu as pltpu
from jax.sharding import PartitionSpec as P


LANES = 128
BF16 = jnp.bfloat16
F32 = jnp.float32
MIB = 1 << 20
NEAR, FAR = 3, 2
HBM = pl.BlockSpec(memory_space=pltpu.HBM)
VMEM = pl.BlockSpec(memory_space=pltpu.VMEM)
SMEM = pl.BlockSpec(memory_space=pltpu.SMEM)


def in_hbm(array):
    return pltpu.with_memory_space_constraint(array, pltpu.HBM)


def swap(array, axis, bit):
    size = lax.axis_size(axis)
    return lax.ppermute(array, axis, [(i, i ^ bit) for i in range(size)])


def mask_row(ranks, tile, rank_width):
    start = tile * LANES
    freq = start // rank_width
    offset = start - freq * rank_width
    following = jnp.minimum(freq + 1, ranks.shape[0] - 1)
    step = offset + lax.broadcasted_iota(jnp.int32, (1, LANES), 1)
    limit = jnp.where(step < rank_width, ranks[freq], ranks[following] + rank_width)
    return jnp.where(step < limit, 1.0, 0.0).astype(F32)


def both_parts(rows):
    half = rows.shape[0] // 2
    re, im = rows[:half, :], rows[half:, :]
    return (
        jnp.concatenate([re, im], axis=1),
        jnp.concatenate([im, -re], axis=1),
    )


def add_products(rows, basis, out, first):
    half = out.shape[0] // 2
    width = min(2 * LANES, out.shape[1])
    for index, left in enumerate(both_parts(rows)):
        for low in range(0, out.shape[1], width):
            place = (slice(index * half, (index + 1) * half), slice(low, low + width))
            right = basis[:, :, low : low + width].reshape(-1, width)
            product = jnp.dot(left, right, preferred_element_type=F32)
            if first:
                out[place] = product
            else:
                out[place] += product


def first_kernel(ranks, where, vis, basis, rows_out, send, rows, vis_held, basis_held, sems, *, chunk, rank_width):
    columns, width = basis_held.shape[1:]
    tiles = chunk // LANES
    chunks = columns // chunk
    half = rows.shape[0] // 2
    first_mode = pl.multiple_of(where[0] * width, width)
    copies = []
    for i in range(chunks):
        these = pl.ds(i * chunk, chunk)
        some = pl.ds(i * tiles, tiles)
        arrivals = [
            pltpu.make_async_copy(
                vis.at[:, :, k, some], vis_held.at[:, :, some, k], sems.at[i, k]
            )
            for k in range(4)
        ]
        arrivals.append(
            pltpu.make_async_copy(
                basis.at[:, these, pl.ds(first_mode, width)],
                basis_held.at[:, these, :],
                sems.at[i, 4],
            )
        )
        for copy in arrivals:
            copy.start()
        sent = pltpu.make_async_copy(rows.at[:, these], rows_out.at[:, these], sems.at[i, 5])
        copies.append((arrivals, sent))
    flat = vis_held.reshape(2, vis_held.shape[1], columns // LANES, 8, LANES)

    def mask_chunk(i):
        for copy in copies[i][0][:4]:
            copy.wait()
        for tile in range(i * tiles, (i + 1) * tiles):
            mask = mask_row(ranks, tile, rank_width)
            for part in range(2):
                block = flat[part, :, tile].reshape(half, LANES) * mask
                rows[part * half : (part + 1) * half, tile * LANES : (tile + 1) * LANES] = (
                    block.astype(BF16)
                )

    mask_chunk(0)
    for i in range(chunks):
        if i + 1 < chunks:
            mask_chunk(i + 1)
        copies[i][0][4].wait()
        copies[i][1].start()
        lanes = slice(i * chunk, (i + 1) * chunk)
        add_products(rows.at[:, lanes], basis_held.at[:, lanes, :], send, i == 0)
    for _, sent in copies:
        sent.wait()


def project_first(vis, ranks, where, basis, width):
    _, reals, _, columns = vis.shape
    chunk = 4 * LANES
    view = vis.reshape(2, reals // 4, 4, 2, columns // LANES, LANES).transpose(0, 1, 2, 4, 3, 5)
    rows = 2 * reals
    return pl.pallas_call(
        functools.partial(first_kernel, chunk=chunk, rank_width=columns // ranks.shape[0]),
        in_specs=[SMEM, SMEM, HBM, HBM],
        out_specs=[HBM, VMEM],
        scratch_shapes=[
            pltpu.VMEM((2 * rows, columns), BF16),
            pltpu.VMEM((2, reals // 4, columns // LANES, 4, 2, LANES), F32),
            pltpu.VMEM((2, columns, width), BF16),
            pltpu.SemaphoreType.DMA((columns // chunk, 6)),
        ],
        out_shape=[
            pltpu.HBM((2 * rows, columns), BF16),
            jax.ShapeDtypeStruct((2 * rows, width), F32),
        ],
        compiler_params=pltpu.CompilerParams(vmem_limit_bytes=24 * MIB),
        cost_estimate=pl.CostEstimate(
            flops=8 * rows * columns * width,
            bytes_accessed=vis.size * 4 + columns * width * 4 + rows * columns * 4,
            transcendentals=0,
        ),
        name="project_first",
    )(in_hbm(ranks), where, in_hbm(view), in_hbm(basis))


def again_kernel(where, rows, basis, out, rows_held, basis_held, sems):
    columns, width = basis_held.shape[1:]
    chunks = sems.shape[0]
    chunk = columns // chunks
    first_mode = pl.multiple_of(where[0] * width, width)
    copies = []
    for i in range(chunks):
        these = pl.ds(i * chunk, chunk)
        copies.append(
            (
                pltpu.make_async_copy(rows.at[:, these], rows_held.at[:, these], sems.at[i, 0]),
                pltpu.make_async_copy(
                    basis.at[:, these, pl.ds(first_mode, width)],
                    basis_held.at[:, these, :],
                    sems.at[i, 1],
                ),
            )
        )
        for copy in copies[-1]:
            copy.start()
    for i in range(chunks):
        for copy in copies[i]:
            copy.wait()
        lanes = slice(i * chunk, (i + 1) * chunk)
        add_products(rows_held.at[:, lanes], basis_held.at[:, lanes, :], out, i == 0)


def project_again(rows, where, basis, width):
    rows2, columns = rows.shape
    return pl.pallas_call(
        again_kernel,
        in_specs=[SMEM, HBM, HBM],
        out_specs=VMEM,
        scratch_shapes=[
            pltpu.VMEM((rows2, columns), BF16),
            pltpu.VMEM((2, columns, width), BF16),
            pltpu.SemaphoreType.DMA((columns // (4 * LANES), 2)),
        ],
        out_shape=jax.ShapeDtypeStruct((rows2, width), F32),
        compiler_params=pltpu.CompilerParams(vmem_limit_bytes=12 * MIB),
        cost_estimate=pl.CostEstimate(
            flops=4 * rows2 * columns * width,
            bytes_accessed=rows.size * 2 + columns * width * 4,
            transcendentals=0,
        ),
        name="project_again",
    )(where, in_hbm(rows), in_hbm(basis))


def weight_kernel(own, core_part, chip_part, weights, out, *, blocks):
    rows = own.shape[0] // 2
    per = rows // blocks
    for part in range(2):
        for block in range(blocks):
            these = slice(part * rows + block * per, part * rows + (block + 1) * per)
            total = own[these, :] + core_part[these, :] + chip_part[these, :].astype(F32)
            factor = weights[block * per : (block + 1) * per, :]
            out[block, part * per : (part + 1) * per, :] = (total * factor).astype(BF16)


def apply_weights(own, core_half, where, chip_part, weights, blocks):
    rows, width = own.shape
    per = rows // blocks
    return pl.pallas_call(
        lambda w, *refs: weight_kernel(*refs, blocks=blocks),
        grid_spec=pltpu.PrefetchScalarGridSpec(
            num_scalar_prefetch=1,
            grid=(1,),
            in_specs=[
                pl.BlockSpec((rows, width), lambda i, w: (0, 0)),
                pl.BlockSpec((rows, width), lambda i, w: (0, w[0])),
                pl.BlockSpec((rows, width), lambda i, w: (0, 0)),
                pl.BlockSpec(weights.shape, lambda i, w: (0, 0)),
            ],
            out_specs=pl.BlockSpec((blocks, per, width), lambda i, w: (0, 0, 0)),
        ),
        out_shape=jax.ShapeDtypeStruct((blocks, per, width), BF16),
        compiler_params=pltpu.CompilerParams(vmem_limit_bytes=8 * MIB),
        name="apply_weights",
    )(where, own, core_half, chip_part, weights)


def add_kernel(w, own, core_part, out):
    out[...] = (own[...] + core_part[...]).astype(BF16)


def add_parts(own, core_half, where):
    rows, width = own.shape
    return pl.pallas_call(
        add_kernel,
        grid_spec=pltpu.PrefetchScalarGridSpec(
            num_scalar_prefetch=1,
            grid=(1,),
            in_specs=[
                pl.BlockSpec((rows, width), lambda i, w: (0, 0)),
                pl.BlockSpec((rows, width), lambda i, w: (0, w[0])),
            ],
            out_specs=pl.BlockSpec((rows, width), lambda i, w: (0, 0)),
        ),
        out_shape=jax.ShapeDtypeStruct((rows, width), BF16),
        compiler_params=pltpu.CompilerParams(vmem_limit_bytes=8 * MIB),
        name="add_parts",
    )(where, own, core_half)


def butterfly(a, b, c, d):
    s_re, s_im = a[0] + c[0], a[1] + c[1]
    d_re, d_im = a[0] - c[0], a[1] - c[1]
    t_re, t_im = b[0] + d[0], b[1] + d[1]
    e_re, e_im = b[0] - d[0], b[1] - d[1]
    return (
        (s_re + t_re, s_im + t_im),
        (d_re - e_im, d_im + e_re),
        (s_re - t_re, s_im - t_im),
        (d_re + e_im, d_im - e_re),
    )


def twiddle(value, index, scale):
    re, im = value
    quarter = index % 16
    cosine = math.cos(2 * math.pi * quarter / 16) * scale
    sine = math.sin(2 * math.pi * quarter / 16) * scale
    if quarter == 0:
        return (re * scale, im * scale)
    if quarter == 4:
        return (im * -scale, re * scale)
    if quarter == 2:
        return ((re - im) * cosine, (re + im) * cosine)
    if quarter == 6:
        return ((re + im) * cosine, (re - im) * sine)
    return (re * cosine - im * sine, re * sine + im * cosine)


def transform(values):
    inner = []
    for m1 in range(4):
        outs = butterfly(*[values[m1 + 4 * m0] for m0 in range(4)])
        inner.append([twiddle(outs[t0], m1 * t0, 0.25) for t0 in range(4)])
    result = [None] * 16
    for t0 in range(4):
        outs = butterfly(*[inner[m1][t0] for m1 in range(4)])
        for t1 in range(4):
            result[4 * t1 + t0] = outs[t1]
    return result


def transform_kernel(coeffs, out, held, moved):
    blocks, per4, width = coeffs.shape
    per = per4 // 4
    points = 2 * blocks
    rows = per * points
    for lane_tile in range(width // LANES):
        lanes = slice(lane_tile * LANES, (lane_tile + 1) * LANES)
        for block in range(blocks):
            held[lane_tile, block * per4 : (block + 1) * per4, :] = coeffs[block, :, lanes].astype(F32)
        loaded = []
        for m in range(points):
            start = m // 2 * per4 + m % 2
            loaded.append(
                [
                    held[lane_tile, pl.ds(start + part * 2 * per, per, stride=2), :]
                    for part in range(2)
                ]
            )
        result = transform(loaded)
        for t in range(points):
            for part in range(2):
                moved[lane_tile, pl.ds(part * rows + t, per, stride=points), :] = result[t][part]
        for part in range(2):
            out[part, :, lanes] = moved[lane_tile, part * rows : (part + 1) * rows, :].astype(BF16)


def to_times(coeffs):
    blocks, per4, width = coeffs.shape
    rows = blocks * per4 // 2
    return pl.pallas_call(
        transform_kernel,
        in_specs=[VMEM],
        out_specs=VMEM,
        scratch_shapes=[pltpu.VMEM((width // LANES, 2 * rows, LANES), F32)] * 2,
        out_shape=jax.ShapeDtypeStruct((2, rows, width), BF16),
        compiler_params=pltpu.CompilerParams(vmem_limit_bytes=8 * MIB),
        name="to_times",
    )(coeffs)


def place_rows(rows, coeffs):
    half = rows.shape[0] // 2
    for piece, coeff in enumerate(coeffs):
        width = coeff.shape[2]
        first = slice(2 * piece * width, (2 * piece + 1) * width)
        second = slice((2 * piece + 1) * width, (2 * piece + 2) * width)
        re, im = coeff[0], coeff[1]
        rows[:half, first] = re
        rows[:half, second] = -im
        rows[half:, first] = im
        rows[half:, second] = re


def start_basis(where, basis, held, sems, tile_index, pieces):
    _, tile, width = held.shape[2:]
    copies = []
    for piece in pieces:
        first_mode = pl.multiple_of(where[piece] * width, width)
        copy = pltpu.make_async_copy(
            basis.at[:, pl.ds(tile_index * tile, tile), pl.ds(first_mode, width)],
            held.at[tile_index, piece],
            sems.at[tile_index, piece],
        )
        copy.start()
        copies.append(copy)
    return copies


def field_parts(rows, held, tile_index, pieces):
    right = jnp.concatenate(
        [held[tile_index, piece, part] for piece in pieces for part in range(2)], axis=1
    )
    half = rows.shape[0] // 2
    depth = held.shape[4] * 2
    lanes = slice(pieces[0] * depth, (pieces[-1] + 1) * depth)
    for part in range(2):
        yield part, lax.dot_general(
            rows[part * half : (part + 1) * half, lanes],
            right,
            (((1,), (1,)), ((), ())),
            preferred_element_type=F32,
        )


def part_kernel(where, *refs, pieces, near):
    coeffs = refs[:pieces]
    basis, *refs = refs[pieces:]
    kept, (far, rows, held, staged, sems) = refs[:near], refs[near:]
    every = range(pieces)
    tiles = held.shape[0]
    order = [*range(near, tiles), *range(near)]
    copies = {i: start_basis(where, basis, held, sems, i, every) for i in order}
    place_rows(rows, coeffs)
    sends = []
    for i in order:
        for copy in copies[i]:
            copy.wait()
        target = kept[i] if i < near else staged.at[i - near]
        for part, value in field_parts(rows, held, i, every):
            target[part] = value
        if i >= near:
            copy = pltpu.make_async_copy(staged.at[i - near], far.at[i - near], sems.at[i, pieces])
            copy.start()
            sends.append(copy)
    for copy in sends:
        copy.wait()


def make_part(coeffs, where, basis, tile, near, far):
    pieces = len(coeffs)
    _, rows, width = coeffs[0].shape
    part = (2, rows, tile)
    tiles = near + far
    return pl.pallas_call(
        functools.partial(part_kernel, pieces=pieces, near=near),
        in_specs=[SMEM] + [VMEM] * pieces + [HBM],
        out_specs=[VMEM] * near + [HBM],
        scratch_shapes=[
            pltpu.VMEM((2 * rows, 2 * pieces * width), BF16),
            pltpu.VMEM((tiles, pieces, 2, tile, width), BF16),
            pltpu.VMEM((far, *part), F32),
            pltpu.SemaphoreType.DMA((tiles, pieces + 1)),
        ],
        out_shape=[jax.ShapeDtypeStruct(part, F32)] * near + [pltpu.HBM((far, *part), F32)],
        compiler_params=pltpu.CompilerParams(vmem_limit_bytes=16 * MIB),
        cost_estimate=pl.CostEstimate(
            flops=8 * rows * tiles * tile * width * pieces,
            bytes_accessed=tiles * tile * width * pieces * 4,
            transcendentals=0,
        ),
        name="make_part",
    )(where, *coeffs, in_hbm(basis))


def series_kernel(where, *refs, pieces, old):
    coeffs = refs[:pieces]
    basis, *partial = refs[pieces:-6]
    far = partial.pop()
    out, rows, held, staged, series, sems = refs[-6:]
    tiles, _, _, tile, _ = held.shape
    near = len(partial)
    done = near + staged.shape[0]
    copies, sends = [], []
    for i in range(tiles):
        used = range(old if i < done else 0, pieces)
        copies.append((used, start_basis(where, basis, held, sems, i, used)))
        if near <= i < done:
            copy = pltpu.make_async_copy(far.at[i - near], staged.at[i - near], sems.at[i, pieces])
            copy.start()
            copies[i][1].append(copy)
    place_rows(rows, coeffs)
    for i, (used, arrivals) in enumerate(copies):
        for copy in arrivals:
            copy.wait()
        for part, value in field_parts(rows, held, i, used):
            if i < near:
                value += partial[i][part]
            elif i < done:
                value += staged[i - near, part]
            series[i, part] = value
        copy = pltpu.make_async_copy(
            series.at[i], out.at[:, :, pl.ds(i * tile, tile)], sems.at[i, pieces + 1]
        )
        copy.start()
        sends.append(copy)
    for copy in sends:
        copy.wait()


def make_series(coeffs, where, basis, tile, partial, old):
    pieces = len(coeffs)
    _, rows, width = coeffs[0].shape
    columns = basis.shape[1]
    tiles = columns // tile
    return pl.pallas_call(
        functools.partial(series_kernel, pieces=pieces, old=old),
        in_specs=[SMEM] + [VMEM] * pieces + [HBM] + [VMEM] * (len(partial) - 1) + [HBM],
        out_specs=HBM,
        scratch_shapes=[
            pltpu.VMEM((2 * rows, 2 * pieces * width), BF16),
            pltpu.VMEM((tiles, pieces, 2, tile, width), BF16),
            pltpu.VMEM(partial[-1].shape, F32),
            pltpu.VMEM((tiles, 2, rows, tile), F32),
            pltpu.SemaphoreType.DMA((tiles, pieces + 2)),
        ],
        out_shape=jax.ShapeDtypeStruct((2, rows, columns), F32),
        compiler_params=pltpu.CompilerParams(vmem_limit_bytes=36 * MIB),
        cost_estimate=pl.CostEstimate(
            flops=8 * rows * columns * width * pieces,
            bytes_accessed=columns * width * pieces * 4 + rows * columns * 8,
            transcendentals=0,
        ),
        name="make_series",
    )(where, *coeffs, in_hbm(basis), *partial[:-1], in_hbm(partial[-1]))


def fast_shards(visibility, svd_ranks, kl_basis, weight_table, seed_labels):
    _, reals, _, columns = visibility.shape
    modes = kl_basis.shape[2]
    blocks = lax.axis_size("ma")
    index = lax.axis_index("freq")
    core, chip = index & 1, index >> 1
    half, width = modes // 2, modes // 4
    mine = core * 2 + chip
    one = lambda value: value[None].astype(jnp.int32)

    rows, away = project_first(visibility, svd_ranks, one(1 - core), kl_basis, half)
    core_half = swap(away, "freq", 1)
    chip_own = project_again(rows, one(core * 2 + 1 - chip), kl_basis, width)
    chip_send = add_parts(chip_own, core_half, one(1 - chip))
    chip_part = swap(chip_send, "freq", 2)
    own = project_again(rows, one(mine), kl_basis, width)

    table = lax.dynamic_slice_in_dim(weight_table, mine * width, width, 1)
    sets = jnp.arange(weight_table.shape[0], dtype=jnp.int32)
    one_hot = (jnp.repeat(seed_labels, 2)[:, None] == sets[None, :]).astype(F32)
    weights = jnp.dot(one_hot, table, precision=lax.Precision.HIGHEST)
    coeffs = apply_weights(own, core_half, one(chip), chip_part, weights, blocks)

    coeffs = lax.all_to_all(coeffs, "ma", split_axis=0, concat_axis=0, tiled=True)
    coeffs = to_times(coeffs)
    from_core = swap(coeffs, "freq", 1)
    from_chip = swap(coeffs, "freq", 2)
    places = jnp.stack(
        [mine, (1 - core) * 2 + chip, core * 2 + 1 - chip, (1 - core) * 2 + 1 - chip]
    ).astype(jnp.int32)
    tile = 4 * LANES
    partial = make_part([coeffs, from_core], places, kl_basis, tile, NEAR, FAR)
    from_chip, partial = lax.optimization_barrier((from_chip, partial))
    from_both = swap(from_chip, "freq", 1)
    series = make_series(
        [coeffs, from_core, from_chip, from_both], places, kl_basis, tile, partial, 2
    )
    return series.reshape(2, reals // blocks, 2 * blocks, columns)


def plain_shards(visibility, svd_ranks, kl_basis, weight_table, seed_labels):
    _, reals, local_m, columns = visibility.shape
    rank_width = columns // svd_ranks.shape[0]
    steps = jnp.arange(rank_width, dtype=jnp.int32)
    mask = (steps[None, :] < svd_ranks[:, None]).astype(F32).reshape(1, 1, 1, columns)
    masked = (visibility * mask).astype(BF16).reshape(2, reals * local_m, columns)

    def product(matrix, signal):
        return lax.dot_general(
            matrix, signal, (((0,), (1,)), ((), ())), preferred_element_type=F32
        )

    modes_re = product(kl_basis[0], masked[0]) + product(kl_basis[1], masked[1])
    modes_im = product(kl_basis[0], masked[1]) - product(kl_basis[1], masked[0])
    parts = jnp.stack([modes_re, modes_im], axis=1)
    summed = lax.psum_scatter(parts, "freq", scatter_dimension=0, tiled=True)
    held = summed.shape[0]
    table = lax.dynamic_slice_in_dim(weight_table, lax.axis_index("freq") * held, held, 1)
    labels = jnp.repeat(seed_labels, local_m)
    sets = jnp.arange(weight_table.shape[0], dtype=jnp.int32)
    one_hot = (sets[:, None] == labels[None, :]).astype(F32)
    weights = lax.dot_general(
        table, one_hot, (((0,), (0,)), ((), ())), precision=lax.Precision.HIGHEST
    )
    coeffs = (summed * weights[:, None, :]).astype(BF16)
    coeffs = lax.all_to_all(
        coeffs.reshape(held, 2, reals, local_m), "ma", split_axis=2, concat_axis=3, tiled=True
    ).reshape(held, 2, -1)
    coeffs = lax.all_gather(coeffs, "freq", axis=0, tiled=True)
    fields_re = product(coeffs[:, 0], kl_basis[0]) - product(coeffs[:, 1], kl_basis[1])
    fields_im = product(coeffs[:, 0], kl_basis[1]) + product(coeffs[:, 1], kl_basis[0])
    shape = (reals // lax.axis_size("ma"), -1, columns)
    fields_re, fields_im = fields_re.reshape(shape), fields_im.reshape(shape)
    length = fields_re.shape[1]
    index = jnp.arange(length, dtype=jnp.int32)
    angles = (index[:, None] * index[None, :] % length).astype(F32) * (2.0 * math.pi / length)
    cosine = jnp.cos(angles) / math.sqrt(length)
    sine = jnp.sin(angles) / math.sqrt(length)

    def apply(matrix, signal):
        return jnp.einsum("tm,rmc->rtc", matrix, signal, precision=lax.Precision.HIGHEST)

    return jnp.stack(
        [
            apply(cosine, fields_re) - apply(sine, fields_im),
            apply(sine, fields_re) + apply(cosine, fields_im),
        ]
    )


def fits(mesh, visibility, svd_ranks, kl_basis):
    blocks, freq = mesh.shape["ma"], mesh.shape["freq"]
    _, reals, points, columns = visibility.shape
    rank_width = columns // svd_ranks.shape[0]
    return (
        freq == 4
        and points == 16
        and points == 2 * blocks
        and reals % (16 * blocks) == 0
        and rank_width >= LANES
        and columns // freq % (4 * LANES) == 0
        and columns // freq // (4 * LANES) >= NEAR + FAR
        and kl_basis.shape[2] % (4 * LANES) == 0
    )


def solution(mesh):
    in_specs = (P(None, None, "ma", "freq"), P("freq"), P(None, "freq", None), P(), P())
    out_specs = P(None, "ma", None, "freq")

    def program(visibility, svd_ranks, kl_basis, weight_table, seed_labels):
        body = fast_shards if fits(mesh, visibility, svd_ranks, kl_basis) else plain_shards
        return jax.shard_map(
            body, mesh=mesh, in_specs=in_specs, out_specs=out_specs, check_vma=False
        )(visibility, svd_ranks, kl_basis, weight_table, seed_labels)

    return program
```

```python
import functools
import math

import jax
import jax.numpy as jnp
from jax import lax
from jax.experimental import pallas as pl
from jax.experimental.pallas import tpu as pltpu
from jax.sharding import PartitionSpec as P


LANES = 128
BF16 = jnp.bfloat16
F32 = jnp.float32
MIB = 1 << 20
CHUNK = 4 * LANES
NEAR_ROWS = 1
NEAR, FAR = 3, 3
HBM = pl.BlockSpec(memory_space=pltpu.HBM)
VMEM = pl.BlockSpec(memory_space=pltpu.VMEM)
SMEM = pl.BlockSpec(memory_space=pltpu.SMEM)


def in_hbm(array):
    return pltpu.with_memory_space_constraint(array, pltpu.HBM)


def swap(array, axis, bit):
    size = lax.axis_size(axis)
    return lax.ppermute(array, axis, [(i, i ^ bit) for i in range(size)])


def mask_row(ranks, tile, rank_width):
    start = tile * LANES
    freq = start // rank_width
    offset = start - freq * rank_width
    following = jnp.minimum(freq + 1, ranks.shape[0] - 1)
    step = offset + lax.broadcasted_iota(jnp.int32, (1, LANES), 1)
    limit = jnp.where(step < rank_width, ranks[freq], ranks[following] + rank_width)
    return jnp.where(step < limit, 1.0, 0.0).astype(F32)


def both_parts(rows):
    half = rows.shape[0] // 2
    re, im = rows[:half, :], rows[half:, :]
    return (
        jnp.concatenate([re, im], axis=1),
        jnp.concatenate([im, -re], axis=1),
    )


def add_products(rows, basis, out, first):
    half = out.shape[0] // 2
    width = min(2 * LANES, out.shape[1])
    for index, left in enumerate(both_parts(rows)):
        for low in range(0, out.shape[1], width):
            place = (slice(index * half, (index + 1) * half), slice(low, low + width))
            right = basis[:, :, low : low + width].reshape(-1, width)
            product = jnp.dot(left, right, preferred_element_type=F32)
            if first:
                out[place] = product
            else:
                out[place] += product


def first_kernel(ranks, where, vis, basis, *refs, chunk, rank_width, near):
    kept, refs = refs[:near], refs[near:]
    far, first_out, second_out, rows, vis_held, basis_held, total, sems = refs
    columns, width = basis_held.shape[1], first_out.shape[1]
    tiles = chunk // LANES
    chunks = columns // chunk
    half = rows.shape[0] // 2
    first_mode = pl.multiple_of(where[0] * 2 * width, 2 * width)
    copies = []
    for i in range(chunks):
        these = pl.ds(i * chunk, chunk)
        some = pl.ds(i * tiles, tiles)
        arrivals = [
            pltpu.make_async_copy(
                vis.at[:, :, k, some], vis_held.at[:, :, some, k], sems.at[i, k]
            )
            for k in range(4)
        ]
        arrivals.append(
            pltpu.make_async_copy(
                basis.at[:, these, pl.ds(first_mode, 2 * width)],
                basis_held.at[:, these, :],
                sems.at[i, 4],
            )
        )
        for copy in arrivals:
            copy.start()
        copies.append(arrivals)
    flat = vis_held.reshape(2, vis_held.shape[1], columns // LANES, 8, LANES)
    sends = []
    for i in range(chunks):
        place = i - (chunks - near)
        source = rows.at[:, i * chunk : (i + 1) * chunk] if place < 0 else kept[place]
        for copy in copies[i][:4]:
            copy.wait()
        for tile in range(tiles):
            mask = mask_row(ranks, i * tiles + tile, rank_width)
            for part in range(2):
                block = flat[part, :, i * tiles + tile].reshape(half, LANES) * mask
                source[part * half : (part + 1) * half, tile * LANES : (tile + 1) * LANES] = (
                    block.astype(BF16)
                )
        copies[i][4].wait()
        if place < 0:
            copy = pltpu.make_async_copy(source, far.at[:, pl.ds(i * chunk, chunk)], sems.at[i, 5])
            copy.start()
            sends.append(copy)
        lanes = slice(i * chunk, (i + 1) * chunk)
        add_products(source, basis_held.at[:, lanes, :], total, i == 0)
    for out, block in ((first_out, where[1]), (second_out, 1 - where[1])):
        out[...] = total[:, pl.ds(pl.multiple_of(block * width, width), width)]
    for copy in sends:
        copy.wait()


def project_first(vis, ranks, where, basis, width, near):
    _, reals, _, columns = vis.shape
    chunk = CHUNK
    view = vis.reshape(2, reals // 4, 4, 2, columns // LANES, LANES).transpose(0, 1, 2, 4, 3, 5)
    rows = 2 * reals
    far = columns - near * chunk
    *kept, spilled, first, second = pl.pallas_call(
        functools.partial(
            first_kernel, chunk=chunk, rank_width=columns // ranks.shape[0], near=near
        ),
        in_specs=[SMEM, SMEM, HBM, HBM],
        out_specs=[VMEM] * near + [HBM, VMEM, VMEM],
        scratch_shapes=[
            pltpu.VMEM((2 * rows, far), BF16),
            pltpu.VMEM((2, reals // 4, columns // LANES, 4, 2, LANES), F32),
            pltpu.VMEM((2, columns, 2 * width), BF16),
            pltpu.VMEM((2 * rows, 2 * width), F32),
            pltpu.SemaphoreType.DMA((columns // chunk, 6)),
        ],
        out_shape=[jax.ShapeDtypeStruct((2 * rows, chunk), BF16)] * near
        + [pltpu.HBM((2 * rows, far), BF16)]
        + [jax.ShapeDtypeStruct((2 * rows, width), F32)] * 2,
        compiler_params=pltpu.CompilerParams(vmem_limit_bytes=24 * MIB),
        cost_estimate=pl.CostEstimate(
            flops=16 * rows * columns * width,
            bytes_accessed=vis.size * 4 + columns * width * 8 + rows * columns * 2,
            transcendentals=0,
        ),
        name="project_first",
    )(in_hbm(ranks), where, in_hbm(view), in_hbm(basis))
    return [*kept, spilled], first, second


def again_kernel(where, *refs):
    *kept, far, basis, out, rows_held, basis_held, sems = refs
    columns, width = basis_held.shape[1:]
    chunks = sems.shape[0]
    chunk = columns // chunks
    spilled = chunks - len(kept)
    first_mode = pl.multiple_of(where[0] * width, width)
    order = [*range(spilled, chunks), *range(spilled)]
    copies = {}
    for i in order:
        these = pl.ds(i * chunk, chunk)
        copies[i] = [
            pltpu.make_async_copy(
                basis.at[:, these, pl.ds(first_mode, width)],
                basis_held.at[:, these, :],
                sems.at[i, 0],
            )
        ]
        if i < spilled:
            copies[i].append(
                pltpu.make_async_copy(far.at[:, these], rows_held.at[:, these], sems.at[i, 1])
            )
        for copy in copies[i]:
            copy.start()
    for i in order:
        for copy in copies[i]:
            copy.wait()
        lanes = slice(i * chunk, (i + 1) * chunk)
        source = rows_held.at[:, lanes] if i < spilled else kept[i - spilled]
        add_products(source, basis_held.at[:, lanes, :], out, i == order[0])


def project_again(rows, where, basis, width):
    *kept, spilled = rows
    rows2, far = spilled.shape
    columns = basis.shape[1]
    return pl.pallas_call(
        again_kernel,
        in_specs=[SMEM] + [VMEM] * len(kept) + [HBM, HBM],
        out_specs=VMEM,
        scratch_shapes=[
            pltpu.VMEM((rows2, far), BF16),
            pltpu.VMEM((2, columns, width), BF16),
            pltpu.SemaphoreType.DMA((columns // CHUNK, 2)),
        ],
        out_shape=jax.ShapeDtypeStruct((rows2, width), F32),
        compiler_params=pltpu.CompilerParams(vmem_limit_bytes=12 * MIB),
        cost_estimate=pl.CostEstimate(
            flops=4 * rows2 * columns * width,
            bytes_accessed=spilled.size * 2 + columns * width * 4,
            transcendentals=0,
        ),
        name="project_again",
    )(where, *kept, in_hbm(spilled), in_hbm(basis))


def weight_kernel(own, core_part, chip_part, weights, out, *, blocks):
    rows = own.shape[0] // 2
    per = rows // blocks
    for part in range(2):
        for block in range(blocks):
            these = slice(part * rows + block * per, part * rows + (block + 1) * per)
            total = own[these, :] + core_part[these, :] + chip_part[these, :].astype(F32)
            factor = weights[block * per : (block + 1) * per, :]
            out[block, part * per : (part + 1) * per, :] = (total * factor).astype(BF16)


def apply_weights(own, core_part, chip_part, weights, blocks):
    rows, width = own.shape
    return pl.pallas_call(
        functools.partial(weight_kernel, blocks=blocks),
        in_specs=[VMEM] * 4,
        out_specs=VMEM,
        out_shape=jax.ShapeDtypeStruct((blocks, rows // blocks, width), BF16),
        compiler_params=pltpu.CompilerParams(vmem_limit_bytes=8 * MIB),
        name="apply_weights",
    )(own, core_part, chip_part, weights)


def add_kernel(own, core_part, out):
    out[...] = (own[...] + core_part[...]).astype(BF16)


def add_parts(own, core_part):
    return pl.pallas_call(
        add_kernel,
        in_specs=[VMEM, VMEM],
        out_specs=VMEM,
        out_shape=jax.ShapeDtypeStruct(own.shape, BF16),
        compiler_params=pltpu.CompilerParams(vmem_limit_bytes=8 * MIB),
        name="add_parts",
    )(own, core_part)


def butterfly(a, b, c, d):
    s_re, s_im = a[0] + c[0], a[1] + c[1]
    d_re, d_im = a[0] - c[0], a[1] - c[1]
    t_re, t_im = b[0] + d[0], b[1] + d[1]
    e_re, e_im = b[0] - d[0], b[1] - d[1]
    return (
        (s_re + t_re, s_im + t_im),
        (d_re - e_im, d_im + e_re),
        (s_re - t_re, s_im - t_im),
        (d_re + e_im, d_im - e_re),
    )


def twiddle(value, index, scale):
    re, im = value
    quarter = index % 16
    cosine = math.cos(2 * math.pi * quarter / 16) * scale
    sine = math.sin(2 * math.pi * quarter / 16) * scale
    if quarter == 0:
        return (re * scale, im * scale)
    if quarter == 4:
        return (im * -scale, re * scale)
    if quarter == 2:
        return ((re - im) * cosine, (re + im) * cosine)
    if quarter == 6:
        return ((re + im) * cosine, (re - im) * sine)
    return (re * cosine - im * sine, re * sine + im * cosine)


def transform(values):
    inner = []
    for m1 in range(4):
        outs = butterfly(*[values[m1 + 4 * m0] for m0 in range(4)])
        inner.append([twiddle(outs[t0], m1 * t0, 0.25) for t0 in range(4)])
    result = [None] * 16
    for t0 in range(4):
        outs = butterfly(*[inner[m1][t0] for m1 in range(4)])
        for t1 in range(4):
            result[4 * t1 + t0] = outs[t1]
    return result


def transform_kernel(coeffs, out, held, moved):
    blocks, per4, width = coeffs.shape
    per = per4 // 4
    points = 2 * blocks
    rows = per * points
    for lane_tile in range(width // LANES):
        lanes = slice(lane_tile * LANES, (lane_tile + 1) * LANES)
        for block in range(blocks):
            held[lane_tile, block * per4 : (block + 1) * per4, :] = coeffs[block, :, lanes].astype(F32)
        loaded = []
        for m in range(points):
            start = m // 2 * per4 + m % 2
            loaded.append(
                [
                    held[lane_tile, pl.ds(start + part * 2 * per, per, stride=2), :]
                    for part in range(2)
                ]
            )
        result = transform(loaded)
        for t in range(points):
            for part in range(2):
                moved[lane_tile, pl.ds(part * rows + t, per, stride=points), :] = result[t][part]
        for part in range(2):
            out[part, :, lanes] = moved[lane_tile, part * rows : (part + 1) * rows, :].astype(BF16)


def to_times(coeffs):
    blocks, per4, width = coeffs.shape
    rows = blocks * per4 // 2
    return pl.pallas_call(
        transform_kernel,
        in_specs=[VMEM],
        out_specs=VMEM,
        scratch_shapes=[pltpu.VMEM((width // LANES, 2 * rows, LANES), F32)] * 2,
        out_shape=jax.ShapeDtypeStruct((2, rows, width), BF16),
        compiler_params=pltpu.CompilerParams(vmem_limit_bytes=8 * MIB),
        name="to_times",
    )(coeffs)


def place_rows(rows, coeffs):
    half = rows.shape[0] // 2
    for piece, coeff in enumerate(coeffs):
        width = coeff.shape[2]
        first = slice(2 * piece * width, (2 * piece + 1) * width)
        second = slice((2 * piece + 1) * width, (2 * piece + 2) * width)
        re, im = coeff[0], coeff[1]
        rows[:half, first] = re
        rows[:half, second] = -im
        rows[half:, first] = im
        rows[half:, second] = re


def start_basis(where, basis, held, sems, tile_index, pieces):
    _, tile, width = held.shape[2:]
    copies = []
    for piece in pieces:
        first_mode = pl.multiple_of(where[piece] * width, width)
        copy = pltpu.make_async_copy(
            basis.at[:, pl.ds(tile_index * tile, tile), pl.ds(first_mode, width)],
            held.at[tile_index, piece],
            sems.at[tile_index, piece],
        )
        copy.start()
        copies.append(copy)
    return copies


def field_parts(rows, held, tile_index, pieces):
    right = jnp.concatenate(
        [held[tile_index, piece, part] for piece in pieces for part in range(2)], axis=1
    )
    half = rows.shape[0] // 2
    depth = held.shape[4] * 2
    lanes = slice(pieces[0] * depth, (pieces[-1] + 1) * depth)
    for part in range(2):
        yield part, lax.dot_general(
            rows[part * half : (part + 1) * half, lanes],
            right,
            (((1,), (1,)), ((), ())),
            preferred_element_type=F32,
        )


def part_kernel(where, *refs, pieces, near):
    coeffs = refs[:pieces]
    basis, *refs = refs[pieces:]
    kept, (far, rows, held, staged, sems) = refs[:near], refs[near:]
    every = range(pieces)
    tiles = held.shape[0]
    order = [*range(near, tiles), *range(near)]
    copies = {i: start_basis(where, basis, held, sems, i, every) for i in order}
    place_rows(rows, coeffs)
    sends = []
    for i in order:
        for copy in copies[i]:
            copy.wait()
        target = kept[i] if i < near else staged.at[i - near]
        for part, value in field_parts(rows, held, i, every):
            target[part] = value
        if i >= near:
            copy = pltpu.make_async_copy(staged.at[i - near], far.at[i - near], sems.at[i, pieces])
            copy.start()
            sends.append(copy)
    for copy in sends:
        copy.wait()


def make_part(coeffs, where, basis, tile, near, far):
    pieces = len(coeffs)
    _, rows, width = coeffs[0].shape
    part = (2, rows, tile)
    tiles = near + far
    return pl.pallas_call(
        functools.partial(part_kernel, pieces=pieces, near=near),
        in_specs=[SMEM] + [VMEM] * pieces + [HBM],
        out_specs=[VMEM] * near + [HBM],
        scratch_shapes=[
            pltpu.VMEM((2 * rows, 2 * pieces * width), BF16),
            pltpu.VMEM((tiles, pieces, 2, tile, width), BF16),
            pltpu.VMEM((far, *part), F32),
            pltpu.SemaphoreType.DMA((tiles, pieces + 1)),
        ],
        out_shape=[jax.ShapeDtypeStruct(part, F32)] * near + [pltpu.HBM((far, *part), F32)],
        compiler_params=pltpu.CompilerParams(vmem_limit_bytes=16 * MIB),
        cost_estimate=pl.CostEstimate(
            flops=8 * rows * tiles * tile * width * pieces,
            bytes_accessed=tiles * tile * width * pieces * 4,
            transcendentals=0,
        ),
        name="make_part",
    )(where, *coeffs, in_hbm(basis))


def series_kernel(where, *refs, pieces, old):
    coeffs = refs[:pieces]
    basis, *partial = refs[pieces:-6]
    far = partial.pop()
    out, rows, held, staged, series, sems = refs[-6:]
    tiles, _, _, tile, _ = held.shape
    near = len(partial)
    done = near + staged.shape[0]
    copies, sends = [], []
    for i in range(tiles):
        used = range(old if i < done else 0, pieces)
        copies.append((used, start_basis(where, basis, held, sems, i, used)))
        if near <= i < done:
            copy = pltpu.make_async_copy(far.at[i - near], staged.at[i - near], sems.at[i, pieces])
            copy.start()
            copies[i][1].append(copy)
    place_rows(rows, coeffs)
    for i, (used, arrivals) in enumerate(copies):
        for copy in arrivals:
            copy.wait()
        for part, value in field_parts(rows, held, i, used):
            if i < near:
                value += partial[i][part]
            elif i < done:
                value += staged[i - near, part]
            series[i, part] = value
            copy = pltpu.make_async_copy(
                series.at[i, part],
                out.at[part, :, pl.ds(i * tile, tile)],
                sems.at[i, pieces + 1 + part],
            )
            copy.start()
            sends.append(copy)
    for copy in sends:
        copy.wait()


def make_series(coeffs, where, basis, tile, partial, old):
    pieces = len(coeffs)
    _, rows, width = coeffs[0].shape
    columns = basis.shape[1]
    tiles = columns // tile
    return pl.pallas_call(
        functools.partial(series_kernel, pieces=pieces, old=old),
        in_specs=[SMEM] + [VMEM] * pieces + [HBM] + [VMEM] * (len(partial) - 1) + [HBM],
        out_specs=HBM,
        scratch_shapes=[
            pltpu.VMEM((2 * rows, 2 * pieces * width), BF16),
            pltpu.VMEM((tiles, pieces, 2, tile, width), BF16),
            pltpu.VMEM(partial[-1].shape, F32),
            pltpu.VMEM((tiles, 2, rows, tile), F32),
            pltpu.SemaphoreType.DMA((tiles, pieces + 3)),
        ],
        out_shape=jax.ShapeDtypeStruct((2, rows, columns), F32),
        compiler_params=pltpu.CompilerParams(vmem_limit_bytes=36 * MIB),
        cost_estimate=pl.CostEstimate(
            flops=8 * rows * columns * width * pieces,
            bytes_accessed=columns * width * pieces * 4 + rows * columns * 8,
            transcendentals=0,
        ),
        name="make_series",
    )(where, *coeffs, in_hbm(basis), *partial[:-1], in_hbm(partial[-1]))


def fast_shards(visibility, svd_ranks, kl_basis, weight_table, seed_labels):
    _, reals, _, columns = visibility.shape
    modes = kl_basis.shape[2]
    blocks = lax.axis_size("ma")
    index = lax.axis_index("freq")
    core, chip = index & 1, index >> 1
    width = modes // 4
    mine = core * 2 + chip
    one = lambda value: value[None].astype(jnp.int32)

    theirs = jnp.stack([1 - core, 1 - chip]).astype(jnp.int32)
    rows, away, stay = project_first(visibility, svd_ranks, theirs, kl_basis, width, NEAR_ROWS)
    core_away = swap(away, "freq", 1)
    chip_own = project_again(rows, one(core * 2 + 1 - chip), kl_basis, width)
    chip_send = add_parts(chip_own, core_away)
    chip_part = swap(chip_send, "freq", 2)
    stay, chip_send = lax.optimization_barrier((stay, chip_send))
    core_part = swap(stay, "freq", 1)
    own = project_again(rows, one(mine), kl_basis, width)

    table = lax.dynamic_slice_in_dim(weight_table, mine * width, width, 1)
    sets = jnp.arange(weight_table.shape[0], dtype=jnp.int32)
    one_hot = (jnp.repeat(seed_labels, 2)[:, None] == sets[None, :]).astype(F32)
    weights = jnp.dot(one_hot, table, precision=lax.Precision.HIGHEST)
    coeffs = apply_weights(own, core_part, chip_part, weights, blocks)

    coeffs = lax.all_to_all(coeffs, "ma", split_axis=0, concat_axis=0, tiled=True)
    coeffs = to_times(coeffs)
    from_core = swap(coeffs, "freq", 1)
    from_chip = swap(coeffs, "freq", 2)
    places = jnp.stack(
        [mine, (1 - core) * 2 + chip, core * 2 + 1 - chip, (1 - core) * 2 + 1 - chip]
    ).astype(jnp.int32)
    tile = 4 * LANES
    partial = make_part([coeffs, from_core], places, kl_basis, tile, NEAR, FAR)
    from_chip, partial = lax.optimization_barrier((from_chip, partial))
    from_both = swap(from_chip, "freq", 1)
    series = make_series(
        [coeffs, from_core, from_chip, from_both], places, kl_basis, tile, partial, 2
    )
    return series.reshape(2, reals // blocks, 2 * blocks, columns)


def plain_shards(visibility, svd_ranks, kl_basis, weight_table, seed_labels):
    _, reals, local_m, columns = visibility.shape
    rank_width = columns // svd_ranks.shape[0]
    steps = jnp.arange(rank_width, dtype=jnp.int32)
    mask = (steps[None, :] < svd_ranks[:, None]).astype(F32).reshape(1, 1, 1, columns)
    masked = (visibility * mask).astype(BF16).reshape(2, reals * local_m, columns)

    def product(matrix, signal):
        return lax.dot_general(
            matrix, signal, (((0,), (1,)), ((), ())), preferred_element_type=F32
        )

    modes_re = product(kl_basis[0], masked[0]) + product(kl_basis[1], masked[1])
    modes_im = product(kl_basis[0], masked[1]) - product(kl_basis[1], masked[0])
    parts = jnp.stack([modes_re, modes_im], axis=1)
    summed = lax.psum_scatter(parts, "freq", scatter_dimension=0, tiled=True)
    held = summed.shape[0]
    table = lax.dynamic_slice_in_dim(weight_table, lax.axis_index("freq") * held, held, 1)
    labels = jnp.repeat(seed_labels, local_m)
    sets = jnp.arange(weight_table.shape[0], dtype=jnp.int32)
    one_hot = (sets[:, None] == labels[None, :]).astype(F32)
    weights = lax.dot_general(
        table, one_hot, (((0,), (0,)), ((), ())), precision=lax.Precision.HIGHEST
    )
    coeffs = (summed * weights[:, None, :]).astype(BF16)
    coeffs = lax.all_to_all(
        coeffs.reshape(held, 2, reals, local_m), "ma", split_axis=2, concat_axis=3, tiled=True
    ).reshape(held, 2, -1)
    coeffs = lax.all_gather(coeffs, "freq", axis=0, tiled=True)
    fields_re = product(coeffs[:, 0], kl_basis[0]) - product(coeffs[:, 1], kl_basis[1])
    fields_im = product(coeffs[:, 0], kl_basis[1]) + product(coeffs[:, 1], kl_basis[0])
    shape = (reals // lax.axis_size("ma"), -1, columns)
    fields_re, fields_im = fields_re.reshape(shape), fields_im.reshape(shape)
    length = fields_re.shape[1]
    index = jnp.arange(length, dtype=jnp.int32)
    angles = (index[:, None] * index[None, :] % length).astype(F32) * (2.0 * math.pi / length)
    cosine = jnp.cos(angles) / math.sqrt(length)
    sine = jnp.sin(angles) / math.sqrt(length)

    def apply(matrix, signal):
        return jnp.einsum("tm,rmc->rtc", matrix, signal, precision=lax.Precision.HIGHEST)

    return jnp.stack(
        [
            apply(cosine, fields_re) - apply(sine, fields_im),
            apply(sine, fields_re) + apply(cosine, fields_im),
        ]
    )


def fits(mesh, visibility, svd_ranks, kl_basis):
    blocks, freq = mesh.shape["ma"], mesh.shape["freq"]
    _, reals, points, columns = visibility.shape
    rank_width = columns // svd_ranks.shape[0]
    return (
        freq == 4
        and points == 16
        and points == 2 * blocks
        and reals % (16 * blocks) == 0
        and rank_width >= LANES
        and columns // freq % (4 * LANES) == 0
        and columns // freq // (4 * LANES) >= max(NEAR + FAR, NEAR_ROWS + 1)
        and kl_basis.shape[2] % (4 * LANES) == 0
    )


def solution(mesh):
    in_specs = (P(None, None, "ma", "freq"), P("freq"), P(None, "freq", None), P(), P())
    out_specs = P(None, "ma", None, "freq")

    def program(visibility, svd_ranks, kl_basis, weight_table, seed_labels):
        body = fast_shards if fits(mesh, visibility, svd_ranks, kl_basis) else plain_shards
        return jax.shard_map(
            body, mesh=mesh, in_specs=in_specs, out_specs=out_specs, check_vma=False
        )(visibility, svd_ranks, kl_basis, weight_table, seed_labels)

    return program
```
